128 devices in a mesh: layer: 16 (over y, z), batch: 8 (over x, core).
Axes of the slice: x: 4, y: 4, z: 4, core: 2. Of those that a mesh axis runs over, the one named last changes fastest.
Arguments:
- inputs: bfloat16 [1024, 4096], P('batch'), may hold values from -6 to 6
- warm_states: bfloat16 [16, 1024, 4096], P('layer', 'batch'), may hold values from -24 to 24
- weights: bfloat16 [64, 32, 4, 128, 128], P('layer'), may hold values from -0.25 to 0.25
- pattern: int32 [64, 32, 4], P('layer'), may hold values from 0 to 31, as said below
- bias: float32 [64, 4096], P('layer'), may hold values from -3 to 3
Outputs:
- ends: bfloat16 [16, 1024, 4096], P('layer', 'batch')
- norms: float32 [2], replicated
The draws below stay inside these ranges and needn't reach their ends.
Inputs may be any that keep to these rules, and one draw needn't show every extreme that they name: `pattern`: for every layer and output block column, the 4 entries are different block indices.
All inputs are finite; a program needn't handle non-finite values.
Results may differ from the reference program's by a relative error of at most 0.04.
Values may be sent and summed in bfloat16 or wider, within the bound.
A program may use at most 128 MiB of HBM per device.

```python
import math
import jax
import jax.numpy as jnp
from jax import lax

D = 4096
BLOCK = 128
LAYERS_DEV = 4
ITERS = 2
NB = 32
KB = 4
BLOCKS = 16
LAYERS = 64
ROWS = 1024


def draw_pattern(key, part):
    keys = jax.random.split(key, LAYERS * NB)
    picks = jax.vmap(lambda single: jax.random.permutation(single, NB)[:KB])(keys)
    return picks.reshape(LAYERS, NB, KB).astype(jnp.int32)


def draw_warm_states(key, part):
    position = jnp.arange(BLOCKS, dtype=jnp.float32) / float(BLOCKS - 1)
    row_place = jnp.arange(ROWS, dtype=jnp.float32) / float(max(ROWS - 1, 1))
    value_key = jax.random.fold_in(key, 11)
    row_key = jax.random.fold_in(key, 23)
    values = jnp.clip(jax.random.normal(value_key, (BLOCKS, ROWS, D), jnp.float32), -5.0, 5.0)
    factor = 1.0 + 2.0 * position
    log_scale = jax.random.uniform(row_key, (ROWS,), jnp.float32, -1.15, 1.15) + math.log(3.0) * (row_place - 0.5)
    scaled = 0.5 * values * factor[:, None, None] * jnp.exp(log_scale)[None, :, None]
    return jnp.clip(scaled, -24.0, 24.0).astype(jnp.bfloat16)


def steps_of(rng, shape, pieces, smallest, largest):
    factor_of, own = 1.0, jax.random.fold_in(rng, 6)
    for dim, shards_of in pieces:
        draws = jnp.exp(jax.random.uniform(jax.random.fold_in(own, dim), (shards_of,), jnp.float32, smallest / len(pieces), largest / len(pieces)))
        factor_of = factor_of * jnp.repeat(draws, shape[dim] // shards_of).reshape([-1 if axis == dim else 1 for axis in range(len(shape))])
    return factor_of


def bell_draw(key, shape, deviation, limit, shards=(), kind=jnp.bfloat16):
    drawn = jax.random.normal(key, shape, jnp.float32) * deviation
    if len(shards) > 0:
        drawn = steps_of(key, shape, shards, -0.22, 0.18) * drawn
    return jnp.clip(drawn, min=-limit, max=limit).astype(kind)


def setup_inputs(seed: int = 0) -> dict:
    seeds = jax.random.split(jax.random.key(seed), 6)
    inputs = bell_draw(seeds[0], (ROWS, D), 1.0, 6.0, ((0, 8),))
    warm_states = draw_warm_states(jax.random.fold_in(seeds[5], 71), 0)
    weights = bell_draw(seeds[2], (LAYERS, NB, KB, BLOCK, BLOCK), (KB * BLOCK) ** -0.5, 0.25, ((0, 16),))
    pattern = draw_pattern(jax.random.fold_in(seeds[5], 71), 0)
    bias = bell_draw(seeds[4], (LAYERS, D), 0.5, 3.0, ((0, 16),), jnp.float32)
    return {"inputs": inputs, "warm_states": warm_states, "weights": weights, "pattern": pattern, "bias": bias}


STEP = 0.25

def preact(state, weight, pattern, bias):
    rows = state.shape[0]
    nblk, kblk, size = (weight.shape[0], weight.shape[1], weight.shape[2])
    blocks = state.reshape(rows, nblk, size)
    picked = jnp.take(blocks, pattern.reshape(-1).astype(jnp.int32), axis=1).reshape(rows, nblk, kblk, size)
    out = jnp.einsum('rnki,nkio->rno', picked.astype(jnp.float32), weight.astype(jnp.float32))
    return out.reshape(rows, nblk * size) + bias

def fine_step(state, weight, pattern, bias):
    return (state.astype(jnp.float32) + STEP * jnp.tanh(preact(state, weight, pattern, bias))).astype(jnp.bfloat16)

def coarse_step(state, weight, pattern, bias):
    return state.astype(jnp.float32) + LAYERS_DEV * STEP * jnp.tanh(preact(state, weight, pattern, bias))

def reference(inputs, warm_states, weights, pattern, bias):
    nblocks = warm_states.shape[0]
    wgrid = weights.reshape((nblocks, LAYERS_DEV) + weights.shape[1:])
    pgrid = pattern.reshape((nblocks, LAYERS_DEV) + pattern.shape[1:])
    bgrid = bias.reshape((nblocks, LAYERS_DEV) + bias.shape[1:])
    ends = warm_states
    norms = []
    for outer in range(ITERS):
        starts = jnp.concatenate([inputs[None], ends[:-1]], axis=0)

        def relax(items):
            start, wblk, pblk, bblk = items
            state = start
            for layer in range(LAYERS_DEV):
                state = fine_step(state, wblk[layer], pblk[layer], bblk[layer])
            tau = state.astype(jnp.float32) - coarse_step(start, wblk[0], pblk[0], bblk[0])
            return (state, tau)
        fine_ends, taus = lax.map(relax, (starts, wgrid, pgrid, bgrid))
        diff = fine_ends.astype(jnp.float32) - ends.astype(jnp.float32)
        norms.append(jnp.sqrt(jnp.sum(diff * diff) / float(diff.size)))

        def advance(carry, items):
            tau, wblk, pblk, bblk = items
            value = (coarse_step(carry, wblk[0], pblk[0], bblk[0]) + tau).astype(jnp.bfloat16)
            return (value, value)
        _, ends = lax.scan(advance, inputs, (taus, wgrid, pgrid, bgrid))
    return (ends, jnp.stack(norms))
```

```python
import functools

import jax
import jax.numpy as jnp
from jax import lax
from jax.experimental import pallas as pl
from jax.experimental.pallas import tpu as pltpu
from jax.sharding import PartitionSpec as P

MESH = pl.DeviceIdType.MESH
STEP = 0.25
ITERS = 2
ROWS = 8
PAIR = 2
BLOCK = 128


def kernel(chain, pat, inputs, warm, weights, bias, out, sums, w, start, own, c1, c2, e1, e2, tau,
           xs, xa, xb, gc, ref, comb, acc, w_sem, own_sem, start_send, start_recv, c1_send, c1_recv,
           c2_send, c2_recv, out_sem):
    me = lax.axis_index("layer")
    nxt, prv = lax.rem(me + 1, chain), lax.rem(me + chain - 1, chain)
    layers, blocks, picks = weights.shape[0], weights.shape[1], 4
    factor = layers * STEP
    chunks = inputs.shape[0]
    pairs = chunks // PAIR
    first, second, last = me == 0, me == 1, me == chain - 1
    rows = PAIR * ROWS

    def to_next(src, dst, send, recv):
        return pltpu.make_async_remote_copy(
            src_ref=src, dst_ref=dst, send_sem=send, recv_sem=recv,
            device_id={"layer": nxt}, device_id_type=MESH)

    def weight_copy(layer):
        return pltpu.make_async_copy(weights.at[layer], w.at[layer], w_sem.at[layer])

    def own_copy(j):
        return pltpu.make_async_copy(warm.at[j], own.at[j], own_sem.at[j])

    def input_copy(j):
        return pltpu.make_async_copy(inputs.at[j], start.at[j], start_recv.at[j])

    def warm_send(j):
        return to_next(warm.at[j], start.at[j], start_send.at[j], start_recv.at[j])

    def c1_copy(j):
        return to_next(e1.at[j], c1.at[j], c1_send.at[j], c1_recv.at[j])

    def c2_copy(j):
        return to_next(e2.at[j], c2.at[j], c2_send.at[j], c2_recv.at[j])

    def out_copy(j, buf):
        return pltpu.make_async_copy(buf.at[j], out.at[j], out_sem.at[j])

    def each(count, do):
        def body(j, carry):
            do(j)
            return carry
        lax.fori_loop(0, count, body, 0)

    weight_copy(0).start()

    @pl.when(first)
    def _():
        each(chunks, lambda j: input_copy(j).start())

    each(chunks, lambda j: own_copy(j).start())
    for layer in range(1, layers):
        weight_copy(layer).start()

    barrier = pltpu.get_barrier_semaphore()
    for neighbour in (nxt, prv):
        pl.semaphore_signal(barrier, inc=1, device_id={"layer": neighbour}, device_id_type=MESH)
    pl.semaphore_wait(barrier, 2)

    @pl.when(jnp.logical_not(last))
    def _():
        each(chunks, lambda j: warm_send(j).start())

    acc[...] = jnp.zeros_like(acc)

    def layer_of(layer, src, epilogue, unroll=True):
        def body(c, carry):
            at = (layer * blocks + c) * picks
            taken = [src[pat[at + k]] for k in range(picks)]
            pre = jnp.dot(jnp.concatenate(taken, axis=1), w[layer, c],
                          preferred_element_type=jnp.float32)
            epilogue(c, jnp.tanh(pre + bias[layer, c]))
            return carry
        lax.fori_loop(0, blocks, body, 0, unroll=unroll)

    def fold(x):
        return jnp.sum(x.reshape(rows // 8, 8, BLOCK), axis=0)

    def relax_first(p):
        for i in range(PAIR):
            j = p * PAIR + i

            @pl.when(first)
            def _():
                input_copy(j).wait()

            @pl.when(jnp.logical_not(first))
            def _():
                warm_send(j).wait_recv()

            own_copy(j).wait()
        x = [start[p * PAIR + i].astype(jnp.float32) for i in range(PAIR)]
        xa[...] = jnp.concatenate(x, axis=1).astype(jnp.bfloat16)
        for i in range(PAIR):
            ref[:, i * ROWS:(i + 1) * ROWS] = own[p * PAIR + i].astype(jnp.float32)

        def epilogue(c, t):
            x = xa[c].astype(jnp.float32)
            gc[c] = x + factor * t
            xb[c] = (x + STEP * t).astype(jnp.bfloat16)
        layer_of(0, xa, epilogue, 16)

    def sweep_first(p):
        def chunk(i, carry):
            j = p * PAIR + i
            c1_copy(j).wait_recv()
            xs[...] = c1[j]
            at_rows = pl.ds(pl.multiple_of(i * ROWS, ROWS), ROWS)

            def epilogue(c, t):
                x = xs[c].astype(jnp.float32)
                coarse = x + factor * t
                end = (coarse + tau[j, c]).astype(jnp.bfloat16)
                e1[j, c] = end
                gc[c, at_rows] = coarse
                ref[c, at_rows] = end.astype(jnp.float32)
                comb[c, at_rows] = x + STEP * t
            layer_of(0, xs, epilogue)

            @pl.when(jnp.logical_not(last))
            def _():
                c1_copy(j).start()
            return carry
        lax.fori_loop(0, PAIR, chunk, 0)
        xb[...] = comb[...].astype(jnp.bfloat16)

    def fine(p, phase):
        src, dst = xb, xa
        for layer in range(1, layers - 1):
            def middle(c, t, src=src, dst=dst):
                dst[c] = (src[c].astype(jnp.float32) + STEP * t).astype(jnp.bfloat16)
            layer_of(layer, src, middle)
            src, dst = dst, src

        def epilogue(c, t):
            g = (src[c].astype(jnp.float32) + STEP * t).astype(jnp.bfloat16).astype(jnp.float32)
            coarse = gc[c]
            correction = g - coarse
            joined = (coarse + correction).astype(jnp.bfloat16).astype(jnp.float32)
            for i in range(PAIR):
                tau[p * PAIR + i, c] = correction[i * ROWS:(i + 1) * ROWS]
            comb[c] = joined
            off = g - ref[c]
            acc[phase] += fold(off * off)
            off = g - joined
            acc[2] += fold(off * off)
        layer_of(layers - 1, src, epilogue)

    def sweep_second(p):
        def chunk(i, carry):
            j = p * PAIR + i
            c2_copy(j).wait_recv()
            xs[...] = c2[j]

            def epilogue(c, t):
                x = xs[c].astype(jnp.float32)
                e2[j, c] = (x + factor * t + tau[j, c]).astype(jnp.bfloat16)
            layer_of(0, xs, epilogue)

            @pl.when(jnp.logical_not(last))
            def _():
                c2_copy(j).start()
            out_copy(j, e2).start()
            return carry
        lax.fori_loop(0, PAIR, chunk, 0)

    for layer in range(layers):
        weight_copy(layer).wait()

    lead = jnp.minimum(pairs, lax.max(me - 1, 0) * 3 // 2)
    lead = jnp.where(first, 0, lead)

    def step(s, carry):
        p = s - lead

        def phase_of(phase, carry):
            run = jnp.where(phase == 0, s < pairs,
                            jnp.logical_and(p >= 0, jnp.logical_not(first)))
            q = jnp.where(phase == 0, s, p)

            @pl.when(run)
            def _():
                @pl.when(phase == 0)
                def _():
                    relax_first(q)

                @pl.when(phase == 1)
                def _():
                    sweep_first(q)

                fine(q, phase)

            return carry
        lax.fori_loop(0, ITERS, phase_of, 0)

        @pl.when(first)
        def _():
            for i in range(PAIR):
                j = s * PAIR + i
                e1[j] = comb[:, i * ROWS:(i + 1) * ROWS].astype(jnp.bfloat16)
                c1_copy(j).start()
                out_copy(j, e1).start()

        @pl.when(second)
        def _():
            for i in range(PAIR):
                j = p * PAIR + i
                e2[j] = comb[:, i * ROWS:(i + 1) * ROWS].astype(jnp.bfloat16)
                c2_copy(j).start()
                out_copy(j, e2).start()

        @pl.when(jnp.logical_and(me >= 2, p >= 0))
        def _():
            sweep_second(p)

        return carry

    lax.fori_loop(0, pairs + lead, step, 0)

    sums[0] = acc[0]
    sums[1] = jnp.where(first, acc[2], acc[1])

    @pl.when(jnp.logical_not(last))
    def _():
        each(chunks, lambda j: warm_send(j).wait_send())
        each(chunks, lambda j: c1_copy(j).wait_send())

    @pl.when(jnp.logical_and(jnp.logical_not(last), jnp.logical_not(first)))
    def _():
        each(chunks, lambda j: c2_copy(j).wait_send())

    each(chunks, lambda j: out_copy(j, e2).wait())


def on_device(inputs, warm_states, weights, pattern, bias):
    chain = lax.axis_size("layer")
    rows, width = inputs.shape
    layers, blocks, picks, size, _ = weights.shape
    chunks = rows // ROWS
    count = float(chain * lax.axis_size("batch") * rows * width)

    def pieces(x):
        return x.reshape(chunks, ROWS, blocks, size).transpose(0, 2, 1, 3)

    any_ = pl.BlockSpec(memory_space=pl.ANY)
    vmem = pl.BlockSpec(memory_space=pltpu.VMEM)
    piece = (chunks, blocks, ROWS, size)
    dma = pltpu.SemaphoreType.DMA
    ends, sums = pl.pallas_call(
        functools.partial(kernel, chain),
        out_shape=(
            jax.ShapeDtypeStruct(piece, jnp.bfloat16),
            jax.ShapeDtypeStruct((ITERS, 8, BLOCK), jnp.float32),
        ),
        in_specs=[pl.BlockSpec(memory_space=pltpu.SMEM), any_, any_, any_, vmem],
        out_specs=(any_, vmem),
        scratch_shapes=[
            pltpu.VMEM((layers, blocks, picks * size, size), jnp.bfloat16),
            *[pltpu.VMEM(piece, jnp.bfloat16)] * 6,
            pltpu.VMEM(piece, jnp.float32),
            pltpu.VMEM((blocks, ROWS, size), jnp.bfloat16),
            *[pltpu.VMEM((blocks, PAIR * ROWS, size), jnp.bfloat16)] * 2,
            *[pltpu.VMEM((blocks, PAIR * ROWS, size), jnp.float32)] * 3,
            pltpu.VMEM((3, 8, BLOCK), jnp.float32),
            dma((layers,)),
            *[dma((chunks,))] * 8,
        ],
        compiler_params=pltpu.CompilerParams(
            collective_id=0, has_side_effects=True, vmem_limit_bytes=60 << 20),
    )(
        pattern.reshape(-1),
        pieces(inputs),
        pieces(warm_states),
        weights.reshape(layers, blocks, picks * size, size),
        bias.reshape(layers, blocks, 1, size),
    )
    total = lax.psum(jnp.sum(sums, axis=(1, 2)), ("layer", "batch"))
    ends = ends.transpose(0, 2, 1, 3).reshape(1, rows, width)
    return ends, jnp.sqrt(total / count)


def solution(mesh):
    in_specs = (
        P("batch", None),
        P("layer", "batch", None),
        P("layer", None, None, None, None),
        P("layer", None, None),
        P("layer", None),
    )
    return jax.shard_map(
        on_device, mesh=mesh, in_specs=in_specs,
        out_specs=(P("layer", "batch", None), P()), check_vma=False)
```

```python
import functools

import jax
import jax.numpy as jnp
from jax import lax
from jax.experimental import pallas as pl
from jax.experimental.pallas import tpu as pltpu
from jax.sharding import PartitionSpec as P

MESH = pl.DeviceIdType.MESH
STEP = 0.25
ITERS = 2
ROWS = 8
PAIR = 2
BLOCK = 128


def kernel(chain, peers, pat, inputs, warm, weights, bias, out, norms, w, start, own, c1, c2, e1, e2, tau,
           xs, xa, xb, gc, ref, comb, acc, part, before, around, total, w_sem, own_sem, start_send, start_recv, c1_send, c1_recv,
           c2_send, c2_recv, out_sem,
           part_send, part_recv, peer_send, peer_recv, total_send, total_recv):
    me = lax.axis_index("layer")
    mine = lax.axis_index("batch")
    nxt, prv = lax.rem(me + 1, chain), lax.rem(me + chain - 1, chain)
    layers, blocks, picks = weights.shape[0], weights.shape[1], 4
    factor = layers * STEP
    chunks = inputs.shape[0]
    pairs = chunks // PAIR
    first, second, last = me == 0, me == 1, me == chain - 1
    rows = PAIR * ROWS

    def to_next(src, dst, send, recv):
        return pltpu.make_async_remote_copy(
            src_ref=src, dst_ref=dst, send_sem=send, recv_sem=recv,
            device_id={"layer": nxt}, device_id_type=MESH)

    def weight_copy(layer):
        return pltpu.make_async_copy(weights.at[layer], w.at[layer], w_sem.at[layer])

    def own_copy(j):
        return pltpu.make_async_copy(warm.at[j], own.at[j], own_sem.at[j])

    def input_copy(j):
        return pltpu.make_async_copy(inputs.at[j], start.at[j], start_recv.at[j])

    def warm_send(j):
        return to_next(warm.at[j], start.at[j], start_send.at[j], start_recv.at[j])

    def c1_copy(j):
        return to_next(e1.at[j], c1.at[j], c1_send.at[j], c1_recv.at[j])

    def c2_copy(j):
        return to_next(e2.at[j], c2.at[j], c2_send.at[j], c2_recv.at[j])

    def part_copy():
        return to_next(part, before, part_send, part_recv)

    def peer_copy(hop):
        return pltpu.make_async_remote_copy(
            src_ref=part, dst_ref=around.at[hop - 1], send_sem=peer_send.at[hop - 1],
            recv_sem=peer_recv.at[hop - 1],
            device_id={"batch": lax.rem(mine + hop, peers)}, device_id_type=MESH)

    def total_copy(layer):
        return pltpu.make_async_remote_copy(
            src_ref=part, dst_ref=total, send_sem=total_send.at[layer], recv_sem=total_recv,
            device_id={"layer": layer}, device_id_type=MESH)

    def out_copy(j, buf):
        return pltpu.make_async_copy(buf.at[j], out.at[j], out_sem.at[j])

    def each(count, do):
        def body(j, carry):
            do(j)
            return carry
        lax.fori_loop(0, count, body, 0)

    weight_copy(0).start()

    @pl.when(first)
    def _():
        each(chunks, lambda j: input_copy(j).start())

    each(chunks, lambda j: own_copy(j).start())
    for layer in range(1, layers):
        weight_copy(layer).start()

    barrier = pltpu.get_barrier_semaphore()

    def greet(**device):
        pl.semaphore_signal(barrier, inc=1, device_id=device, device_id_type=MESH)

    @pl.when(jnp.logical_not(first))
    def _():
        greet(layer=prv)

    @pl.when(jnp.logical_not(last))
    def _():
        greet(layer=chain - 1)
        pl.semaphore_wait(barrier, 1)
        each(chunks, lambda j: warm_send(j).start())

    @pl.when(last)
    def _():
        for hop in range(1, peers):
            greet(batch=lax.rem(mine + hop, peers))
        pl.semaphore_wait(barrier, chain - 1 + peers - 1)

    acc[...] = jnp.zeros_like(acc)

    def layer_of(layer, src, epilogue, unroll=True):
        def body(c, carry):
            taken = [src[pat[layer, k, c]] for k in range(picks)]
            pre = jnp.dot(jnp.concatenate(taken, axis=1), w[layer, c],
                          preferred_element_type=jnp.float32)
            epilogue(c, jnp.tanh(pre + bias[layer:layer + 1, pl.ds(c * BLOCK, BLOCK)]))
            return carry
        lax.fori_loop(0, blocks, body, 0, unroll=unroll)

    def fold(x):
        return jnp.sum(x.reshape(rows // 8, 8, BLOCK), axis=0)

    def relax_first(p):
        for i in range(PAIR):
            j = p * PAIR + i

            @pl.when(first)
            def _():
                input_copy(j).wait()

            @pl.when(jnp.logical_not(first))
            def _():
                warm_send(j).wait_recv()

            own_copy(j).wait()
        x = [start[p * PAIR + i].astype(jnp.float32) for i in range(PAIR)]
        xa[...] = jnp.concatenate(x, axis=1).astype(jnp.bfloat16)
        for i in range(PAIR):
            ref[:, i * ROWS:(i + 1) * ROWS] = own[p * PAIR + i].astype(jnp.float32)

        def epilogue(c, t):
            x = xa[c].astype(jnp.float32)
            gc[c] = x + factor * t
            xb[c] = (x + STEP * t).astype(jnp.bfloat16)
        layer_of(0, xa, epilogue, 16)

    def sweep_first(p):
        def chunk(i, carry):
            j = p * PAIR + i
            c1_copy(j).wait_recv()
            xs[...] = c1[j]
            at_rows = pl.ds(pl.multiple_of(i * ROWS, ROWS), ROWS)

            def epilogue(c, t):
                x = xs[c].astype(jnp.float32)
                coarse = x + factor * t
                end = (coarse + tau[j, c]).astype(jnp.bfloat16)
                e1[j, c] = end
                gc[c, at_rows] = coarse
                ref[c, at_rows] = end.astype(jnp.float32)
                comb[c, at_rows] = x + STEP * t
            layer_of(0, xs, epilogue)

            @pl.when(jnp.logical_not(last))
            def _():
                c1_copy(j).start()
            return carry
        lax.fori_loop(0, PAIR, chunk, 0)
        xb[...] = comb[...].astype(jnp.bfloat16)

    def fine(p, phase):
        src, dst = xb, xa
        for layer in range(1, layers - 1):
            def middle(c, t, src=src, dst=dst):
                dst[c] = (src[c].astype(jnp.float32) + STEP * t).astype(jnp.bfloat16)
            layer_of(layer, src, middle)
            src, dst = dst, src

        def epilogue(c, t):
            g = (src[c].astype(jnp.float32) + STEP * t).astype(jnp.bfloat16).astype(jnp.float32)
            coarse = gc[c]
            correction = g - coarse
            joined = (coarse + correction).astype(jnp.bfloat16).astype(jnp.float32)
            for i in range(PAIR):
                tau[p * PAIR + i, c] = correction[i * ROWS:(i + 1) * ROWS]
            comb[c] = joined
            off = g - ref[c]
            acc[phase] += fold(off * off)
            off = g - joined
            acc[2] += fold(off * off)
        layer_of(layers - 1, src, epilogue)

    def sweep_second(p):
        def chunk(i, carry):
            j = p * PAIR + i
            c2_copy(j).wait_recv()
            xs[...] = c2[j]

            def epilogue(c, t):
                x = xs[c].astype(jnp.float32)
                e2[j, c] = (x + factor * t + tau[j, c]).astype(jnp.bfloat16)
            layer_of(0, xs, epilogue)

            @pl.when(jnp.logical_not(last))
            def _():
                c2_copy(j).start()
            out_copy(j, e2).start()
            return carry
        lax.fori_loop(0, PAIR, chunk, 0)

    for layer in range(layers):
        weight_copy(layer).wait()

    lead = jnp.minimum(pairs, lax.max(me - 1, 0) * 3 // 2)
    lead = jnp.where(first, 0, lead)

    def step(s, carry):
        p = s - lead

        def phase_of(phase, carry):
            run = jnp.where(phase == 0, s < pairs,
                            jnp.logical_and(p >= 0, jnp.logical_not(first)))
            q = jnp.where(phase == 0, s, p)

            @pl.when(run)
            def _():
                @pl.when(phase == 0)
                def _():
                    relax_first(q)

                @pl.when(phase == 1)
                def _():
                    sweep_first(q)

                fine(q, phase)

            return carry
        lax.fori_loop(0, ITERS, phase_of, 0)

        @pl.when(s == pairs + lead - 1)
        def _():
            part[0] = acc[0]
            part[1] = jnp.where(first, acc[2], acc[1])

            @pl.when(jnp.logical_not(first))
            def _():
                part_copy().wait_recv()
                part[...] += before[...]

            @pl.when(jnp.logical_not(last))
            def _():
                part_copy().start()

            @pl.when(last)
            def _():
                for hop in range(1, peers):
                    peer_copy(hop).start()

        @pl.when(first)
        def _():
            for i in range(PAIR):
                j = s * PAIR + i
                e1[j] = comb[:, i * ROWS:(i + 1) * ROWS].astype(jnp.bfloat16)
                c1_copy(j).start()
                out_copy(j, e1).start()

        @pl.when(second)
        def _():
            for i in range(PAIR):
                j = p * PAIR + i
                e2[j] = comb[:, i * ROWS:(i + 1) * ROWS].astype(jnp.bfloat16)
                c2_copy(j).start()
                out_copy(j, e2).start()

        @pl.when(jnp.logical_and(me >= 2, p >= 0))
        def _():
            sweep_second(p)

        return carry

    lax.fori_loop(0, pairs + lead, step, 0)

    @pl.when(last)
    def _():
        for hop in range(1, peers):
            peer_copy(hop).wait()
        part[...] += jnp.sum(around[...], axis=0)
        for layer in range(chain - 1):
            total_copy(layer).start()
        total[...] = part[...]
        for layer in range(chain - 1):
            total_copy(layer).wait_send()

    @pl.when(jnp.logical_not(last))
    def _():
        part_copy().wait_send()
        total_copy(0).wait_recv()
        each(chunks, lambda j: warm_send(j).wait_send())
        each(chunks, lambda j: c1_copy(j).wait_send())

    @pl.when(jnp.logical_and(jnp.logical_not(last), jnp.logical_not(first)))
    def _():
        each(chunks, lambda j: c2_copy(j).wait_send())

    each(chunks, lambda j: out_copy(j, e2).wait())
    for i in range(ITERS):
        norms[i] = jnp.sum(total[i])


def on_device(inputs, warm_states, weights, pattern, bias):
    chain = lax.axis_size("layer")
    rows, width = inputs.shape
    layers, blocks, picks, size, _ = weights.shape
    chunks = rows // ROWS
    count = float(chain * lax.axis_size("batch") * rows * width)

    def pieces(x):
        return x.reshape(chunks, ROWS, blocks, size).transpose(0, 2, 1, 3)

    any_ = pl.BlockSpec(memory_space=pl.ANY)
    vmem = pl.BlockSpec(memory_space=pltpu.VMEM)
    piece = (chunks, blocks, ROWS, size)
    dma = pltpu.SemaphoreType.DMA
    peers = lax.axis_size("batch")
    ends, norms = pl.pallas_call(
        functools.partial(kernel, chain, peers),
        out_shape=(
            jax.ShapeDtypeStruct(piece, jnp.bfloat16),
            jax.ShapeDtypeStruct((ITERS,), jnp.float32),
        ),
        in_specs=[pl.BlockSpec(memory_space=pltpu.SMEM), any_, any_, any_, vmem],
        out_specs=(any_, pl.BlockSpec(memory_space=pltpu.SMEM)),
        scratch_shapes=[
            pltpu.VMEM((layers, blocks, picks * size, size), jnp.bfloat16),
            *[pltpu.VMEM(piece, jnp.bfloat16)] * 6,
            pltpu.VMEM(piece, jnp.float32),
            pltpu.VMEM((blocks, ROWS, size), jnp.bfloat16),
            *[pltpu.VMEM((blocks, PAIR * ROWS, size), jnp.bfloat16)] * 2,
            *[pltpu.VMEM((blocks, PAIR * ROWS, size), jnp.float32)] * 3,
            pltpu.VMEM((3, 8, BLOCK), jnp.float32),
            *[pltpu.VMEM((ITERS, 8, BLOCK), jnp.float32)] * 2,
            pltpu.VMEM((peers - 1, ITERS, 8, BLOCK), jnp.float32),
            pltpu.VMEM((ITERS, 8, BLOCK), jnp.float32),
            dma((layers,)),
            *[dma((chunks,))] * 8,
            dma, dma, dma((peers - 1,)), dma((peers - 1,)), dma((chain - 1,)), dma,
        ],
        compiler_params=pltpu.CompilerParams(
            collective_id=0, has_side_effects=True, vmem_limit_bytes=60 << 20),
    )(
        pattern.transpose(0, 2, 1),
        pieces(inputs),
        pieces(warm_states),
        weights.reshape(layers, blocks, picks * size, size),
        bias,
    )
    ends = ends.transpose(0, 2, 1, 3).reshape(1, rows, width)
    return ends, jnp.sqrt(norms / count)


def solution(mesh):
    in_specs = (
        P("batch", None),
        P("layer", "batch", None),
        P("layer", None, None, None, None),
        P("layer", None, None),
        P("layer", None),
    )
    return jax.shard_map(
        on_device, mesh=mesh, in_specs=in_specs,
        out_specs=(P("layer", "batch", None), P()), check_vma=False)
```

```python
import functools

import jax
import jax.numpy as jnp
from jax import lax
from jax.experimental import pallas as pl
from jax.experimental.pallas import tpu as pltpu
from jax.sharding import PartitionSpec as P

MESH = pl.DeviceIdType.MESH
STEP = 0.25
ITERS = 2
ROWS = 8
PAIR = 2
QUAD = 4
DIRECT = 2
SIDE = 4
BLOCK = 128


def kernel(chain, peers, pat, inputs, warm, weights, bias, out, norms, w, start, own, c1, c2, e1, e2, hold, tau,
           xs, xa, xb, gc, ref, comb, ya, yb, gy, acc, part, before, around, total, w_sem, own_sem, start_send, start_recv,
           hold_send, hold_recv, c1_send, c1_recv,
           c2_send, c2_recv, out_sem,
           part_send, part_recv, peer_send, peer_recv, total_send, total_recv):
    me = lax.axis_index("layer")
    mine = lax.axis_index("batch")
    nxt, prv = lax.rem(me + 1, chain), lax.rem(me + chain - 1, chain)
    layers, blocks, picks = weights.shape[0], weights.shape[1], 4
    factor = layers * STEP
    chunks = inputs.shape[0]
    pairs = chunks // PAIR
    first, second, last = me == 0, me == 1, me == chain - 1
    sender = me < SIDE
    aside = jnp.where(me < SIDE - 1, chain - SIDE + 1 + me, 0)
    late = me > chain - SIDE
    relay = jnp.logical_or(late, first)
    target = jnp.where(first, SIDE, jnp.where(late, me - (chain - SIDE), me))

    def to_next(src, dst, send, recv):
        return pltpu.make_async_remote_copy(
            src_ref=src, dst_ref=dst, send_sem=send, recv_sem=recv,
            device_id={"layer": nxt}, device_id_type=MESH)

    def weight_copy(layer):
        return pltpu.make_async_copy(weights.at[layer], w.at[layer], w_sem.at[layer])

    def pair(ref, p):
        return ref.at[pl.ds(p * PAIR, PAIR)]

    def own_copy(p):
        return pltpu.make_async_copy(pair(warm, p), pair(own, p), own_sem.at[p])

    def input_copy(p):
        return pltpu.make_async_copy(pair(inputs, p), pair(start, p), start_recv.at[p])

    def warm_send(p):
        return to_next(pair(warm, p), pair(start, p), start_send.at[p], start_recv.at[p])

    def warm_aside(p):
        return pltpu.make_async_remote_copy(
            src_ref=pair(warm, p), dst_ref=pair(hold, p), send_sem=start_send.at[p],
            recv_sem=hold_recv.at[p], device_id={"layer": aside}, device_id_type=MESH)

    def warm_back(p):
        return pltpu.make_async_remote_copy(
            src_ref=pair(hold, p), dst_ref=pair(start, p), send_sem=hold_send.at[p],
            recv_sem=start_recv.at[p], device_id={"layer": target}, device_id_type=MESH)

    def c1_copy(j):
        return to_next(e1.at[j], c1.at[j], c1_send.at[j], c1_recv.at[j])

    def c2_copy(j):
        return to_next(e2.at[j], c2.at[j], c2_send.at[j], c2_recv.at[j])

    def part_copy():
        return to_next(part, before, part_send, part_recv)

    def peer_copy(hop):
        return pltpu.make_async_remote_copy(
            src_ref=part, dst_ref=around.at[hop - 1], send_sem=peer_send.at[hop - 1],
            recv_sem=peer_recv.at[hop - 1],
            device_id={"batch": lax.rem(mine + hop, peers)}, device_id_type=MESH)

    def total_copy(layer):
        return pltpu.make_async_remote_copy(
            src_ref=part, dst_ref=total, send_sem=total_send.at[layer], recv_sem=total_recv,
            device_id={"layer": layer}, device_id_type=MESH)

    def out_copy(j, buf):
        return pltpu.make_async_copy(buf.at[j], out.at[j], out_sem.at[j])

    def each(count, do):
        def body(j, carry):
            do(j)
            return carry
        lax.fori_loop(0, count, body, 0)

    weight_copy(0).start()

    @pl.when(first)
    def _():
        each(pairs, lambda p: input_copy(p).start())

    each(pairs, lambda p: own_copy(p).start())
    for layer in range(1, layers):
        weight_copy(layer).start()

    barrier = pltpu.get_barrier_semaphore()

    def greet(**device):
        pl.semaphore_signal(barrier, inc=1, device_id=device, device_id_type=MESH)

    @pl.when(jnp.logical_not(first))
    def _():
        greet(layer=prv)

    @pl.when(jnp.logical_not(last))
    def _():
        greet(layer=chain - 1)

    @pl.when(last)
    def _():
        for hop in range(1, peers):
            greet(batch=lax.rem(mine + hop, peers))

    @pl.when(relay)
    def _():
        greet(layer=jnp.where(first, SIDE - 1, target - 1))

    @pl.when(jnp.logical_and(me >= 1, me <= SIDE))
    def _():
        greet(layer=jnp.where(me == SIDE, 0, me + chain - SIDE))

    def one(flag):
        return jnp.where(flag, 1, 0)

    pl.semaphore_wait(barrier, one(sender) + one(relay)
                      + jnp.where(last, chain - 1 + peers - 1, 1))

    @pl.when(jnp.logical_and(me < chain - SIDE, jnp.logical_not(sender)))
    def _():
        each(pairs, lambda p: warm_send(p).start())

    @pl.when(sender)
    def _():
        each(DIRECT, lambda p: warm_send(p).start())
        each(pairs - DIRECT, lambda p: warm_aside(p + DIRECT).start())

    def pass_on(p):
        warm_aside(p).wait_recv()
        warm_back(p).start()

    @pl.when(late)
    def _():
        each(pairs - DIRECT, lambda p: pass_on(p + DIRECT))

    @pl.when(jnp.logical_and(late, jnp.logical_not(last)))
    def _():
        each(pairs, lambda p: warm_send(p).start())

    acc[...] = jnp.zeros_like(acc)

    def layer_of(layer, src, epilogue, unroll=True):
        def body(c, carry):
            taken = [src[pat[layer, k, c]] for k in range(picks)]
            pre = jnp.dot(jnp.concatenate(taken, axis=1), w[layer, c],
                          preferred_element_type=jnp.float32)
            epilogue(c, jnp.tanh(pre + bias[layer:layer + 1, pl.ds(c * BLOCK, BLOCK)]))
            return carry
        lax.fori_loop(0, blocks, body, 0, unroll=unroll)

    def fold(x):
        return jnp.sum(x.reshape(x.shape[0] // 8, 8, BLOCK), axis=0)

    def fine(src, dst, final):
        for layer in range(1, layers - 1):
            def middle(c, t, src=src, dst=dst):
                dst[c] = (src[c].astype(jnp.float32) + STEP * t).astype(jnp.bfloat16)
            layer_of(layer, src, middle)
            src, dst = dst, src
        layer_of(layers - 1, src, lambda c, t: final(c, src, t))

    def relax_first(q):
        for i in range(QUAD // PAIR):
            p = q * (QUAD // PAIR) + i

            @pl.when(first)
            def _():
                input_copy(p).wait()

            @pl.when(jnp.logical_not(first))
            def _():
                warm_send(p).wait_recv()

            own_copy(p).wait()
        x = [start[q * QUAD + i].astype(jnp.float32) for i in range(QUAD)]
        ya[...] = jnp.concatenate(x, axis=1).astype(jnp.bfloat16)

        def entry(c, t):
            x = ya[c].astype(jnp.float32)
            gy[c] = x + factor * t
            yb[c] = (x + STEP * t).astype(jnp.bfloat16)
        layer_of(0, ya, entry, 16)

        def final(c, src, t):
            g = (src[c].astype(jnp.float32) + STEP * t).astype(jnp.bfloat16).astype(jnp.float32)
            coarse = gy[c]
            correction = g - coarse
            joined = (coarse + correction).astype(jnp.bfloat16)
            for i in range(QUAD):
                j = q * QUAD + i
                at_rows = slice(i * ROWS, (i + 1) * ROWS)
                tau[j, c] = correction[at_rows]
                e1[j, c] = joined[at_rows]
                off = g[at_rows] - own[j, c].astype(jnp.float32)
                acc[0] += off * off
            off = g - joined.astype(jnp.float32)
            acc[2] += fold(off * off)
        fine(yb, ya, final)

    def sweep_first(p):
        def chunk(i, carry):
            j = p * PAIR + i
            c1_copy(j).wait_recv()
            xs[...] = c1[j]
            at_rows = pl.ds(pl.multiple_of(i * ROWS, ROWS), ROWS)

            def epilogue(c, t):
                x = xs[c].astype(jnp.float32)
                coarse = x + factor * t
                end = (coarse + tau[j, c]).astype(jnp.bfloat16)
                e1[j, c] = end
                gc[c, at_rows] = coarse
                ref[c, at_rows] = end.astype(jnp.float32)
                comb[c, at_rows] = x + STEP * t
            layer_of(0, xs, epilogue)

            @pl.when(jnp.logical_not(last))
            def _():
                c1_copy(j).start()
            return carry
        lax.fori_loop(0, PAIR, chunk, 0)
        xb[...] = comb[...].astype(jnp.bfloat16)

        def final(c, src, t):
            g = (src[c].astype(jnp.float32) + STEP * t).astype(jnp.bfloat16).astype(jnp.float32)
            coarse = gc[c]
            correction = g - coarse
            joined = (coarse + correction).astype(jnp.bfloat16)
            for i in range(PAIR):
                j = p * PAIR + i
                at_rows = slice(i * ROWS, (i + 1) * ROWS)
                tau[j, c] = correction[at_rows]
                e2[j, c] = joined[at_rows]
            off = g - ref[c]
            acc[1] += fold(off * off)
        fine(xb, xa, final)

    def sweep_second(p):
        def chunk(i, carry):
            j = p * PAIR + i
            c2_copy(j).wait_recv()
            xs[...] = c2[j]

            def epilogue(c, t):
                x = xs[c].astype(jnp.float32)
                e2[j, c] = (x + factor * t + tau[j, c]).astype(jnp.bfloat16)
            layer_of(0, xs, epilogue)

            @pl.when(jnp.logical_not(last))
            def _():
                c2_copy(j).start()
            out_copy(j, e2).start()
            return carry
        lax.fori_loop(0, PAIR, chunk, 0)

    for layer in range(layers):
        weight_copy(layer).wait()

    quads = chunks // QUAD
    lead = jnp.where(first, quads, jnp.clip(2 * (me - SIDE) + 1, 0, quads))

    def sweeps(p, carry):
        sweep_first(p)

        @pl.when(p == pairs - 1)
        def _():
            gather_part()

        @pl.when(second)
        def _():
            for i in range(PAIR):
                c2_copy(p * PAIR + i).start()
                out_copy(p * PAIR + i, e2).start()

        @pl.when(jnp.logical_not(second))
        def _():
            sweep_second(p)
        return carry

    def gather_part():
        part[0] = acc[0]
        part[1] = jnp.where(first, acc[2], acc[1])

        @pl.when(jnp.logical_not(first))
        def _():
            part_copy().wait_recv()
            part[...] += before[...]

        @pl.when(jnp.logical_not(last))
        def _():
            part_copy().start()

        @pl.when(last)
        def _():
            for hop in range(1, peers):
                peer_copy(hop).start()

    def step(s, carry):
        @pl.when(s < quads)
        def _():
            relax_first(s)

            @pl.when(first)
            def _():
                for i in range(QUAD):
                    c1_copy(s * QUAD + i).start()
                    out_copy(s * QUAD + i, e1).start()
                for i in range(QUAD // PAIR):
                    p = s * (QUAD // PAIR) + i

                    @pl.when(p >= DIRECT)
                    def _():
                        pass_on(p)

        @pl.when(jnp.logical_and(s == quads - 1, me == chain - SIDE))
        def _():
            each(pairs, lambda p: warm_send(p).start())

        @pl.when(jnp.logical_and(s >= lead, jnp.logical_not(first)))
        def _():
            q = s - lead
            lax.fori_loop(q * (QUAD // PAIR), (q + 1) * (QUAD // PAIR), sweeps, 0)

        return carry

    lax.fori_loop(0, jnp.where(first, quads, quads + lead), step, 0)

    @pl.when(first)
    def _():
        gather_part()

    @pl.when(last)
    def _():
        for hop in range(1, peers):
            peer_copy(hop).wait()
        part[...] += jnp.sum(around[...], axis=0)
        for layer in range(chain - 1):
            total_copy(layer).start()
        total[...] = part[...]
        for layer in range(chain - 1):
            total_copy(layer).wait_send()

    @pl.when(jnp.logical_not(last))
    def _():
        part_copy().wait_send()
        total_copy(0).wait_recv()
        each(pairs, lambda p: warm_send(p).wait_send())
        each(chunks, lambda j: c1_copy(j).wait_send())

    @pl.when(jnp.logical_and(jnp.logical_not(last), jnp.logical_not(first)))
    def _():
        each(chunks, lambda j: c2_copy(j).wait_send())

    @pl.when(relay)
    def _():
        each(pairs - DIRECT, lambda p: warm_back(p + DIRECT).wait_send())

    each(chunks, lambda j: out_copy(j, e2).wait())
    for i in range(ITERS):
        norms[i] = jnp.sum(total[i])


def on_device(inputs, warm_states, weights, pattern, bias):
    chain = lax.axis_size("layer")
    rows, width = inputs.shape
    layers, blocks, picks, size, _ = weights.shape
    chunks = rows // ROWS
    count = float(chain * lax.axis_size("batch") * rows * width)

    def pieces(x):
        return x.reshape(chunks, ROWS, blocks, size).transpose(0, 2, 1, 3)

    any_ = pl.BlockSpec(memory_space=pl.ANY)
    vmem = pl.BlockSpec(memory_space=pltpu.VMEM)
    piece = (chunks, blocks, ROWS, size)
    dma = pltpu.SemaphoreType.DMA
    peers = lax.axis_size("batch")
    ends, norms = pl.pallas_call(
        functools.partial(kernel, chain, peers),
        out_shape=(
            jax.ShapeDtypeStruct(piece, jnp.bfloat16),
            jax.ShapeDtypeStruct((ITERS,), jnp.float32),
        ),
        in_specs=[pl.BlockSpec(memory_space=pltpu.SMEM), any_, any_, any_, vmem],
        out_specs=(any_, pl.BlockSpec(memory_space=pltpu.SMEM)),
        scratch_shapes=[
            pltpu.VMEM((layers, blocks, picks * size, size), jnp.bfloat16),
            *[pltpu.VMEM(piece, jnp.bfloat16)] * 7,
            pltpu.VMEM(piece, jnp.float32),
            pltpu.VMEM((blocks, ROWS, size), jnp.bfloat16),
            *[pltpu.VMEM((blocks, PAIR * ROWS, size), jnp.bfloat16)] * 2,
            *[pltpu.VMEM((blocks, PAIR * ROWS, size), jnp.float32)] * 3,
            *[pltpu.VMEM((blocks, QUAD * ROWS, size), jnp.bfloat16)] * 2,
            pltpu.VMEM((blocks, QUAD * ROWS, size), jnp.float32),
            pltpu.VMEM((3, 8, BLOCK), jnp.float32),
            *[pltpu.VMEM((ITERS, 8, BLOCK), jnp.float32)] * 2,
            pltpu.VMEM((peers - 1, ITERS, 8, BLOCK), jnp.float32),
            pltpu.VMEM((ITERS, 8, BLOCK), jnp.float32),
            dma((layers,)),
            *[dma((chunks // PAIR,))] * 5,
            *[dma((chunks,))] * 5,
            dma, dma, dma((peers - 1,)), dma((peers - 1,)), dma((chain - 1,)), dma,
        ],
        compiler_params=pltpu.CompilerParams(
            collective_id=0, has_side_effects=True, vmem_limit_bytes=60 << 20),
    )(
        pattern.transpose(0, 2, 1),
        pieces(inputs),
        pieces(warm_states),
        weights.reshape(layers, blocks, picks * size, size),
        bias,
    )
    ends = ends.transpose(0, 2, 1, 3).reshape(1, rows, width)
    return ends, jnp.sqrt(norms / count)


def solution(mesh):
    in_specs = (
        P("batch", None),
        P("layer", "batch", None),
        P("layer", None, None, None, None),
        P("layer", None, None),
        P("layer", None),
    )
    return jax.shard_map(
        on_device, mesh=mesh, in_specs=in_specs,
        out_specs=(P("layer", "batch", None), P()), check_vma=False)
```

```python
import functools

import jax
import jax.numpy as jnp
from jax import lax
from jax.experimental import pallas as pl
from jax.experimental.pallas import tpu as pltpu
from jax.sharding import PartitionSpec as P

MESH = pl.DeviceIdType.MESH
STEP = 0.25
ITERS = 2
ROWS = 8
PAIR = 2
QUAD = 4
CUT = 2
DIRECT = 2
SIDE = 4
BLOCK = 128


def kernel(chain, peers, pat, inputs, warm, weights, bias, out, norms, w, start, own, c1, c2, e1, e2, hold, tau,
           xs, ya, yb, gc, ref, comb, acc, part, before, around, total, w_sem, own_sem, start_send, start_recv,
           hold_send, hold_recv, c1_send, c1_recv,
           c2_send, c2_recv, out_sem,
           part_send, part_recv, peer_send, peer_recv, total_send, total_recv):
    me = lax.axis_index("layer")
    mine = lax.axis_index("batch")
    nxt, prv = lax.rem(me + 1, chain), lax.rem(me + chain - 1, chain)
    layers, blocks, picks = weights.shape[0], weights.shape[1], 4
    factor = layers * STEP
    chunks = inputs.shape[0]
    pairs = chunks // PAIR
    first, second, last = me == 0, me == 1, me == chain - 1
    quads = chunks // QUAD
    sender = me < SIDE
    aside = jnp.where(me < SIDE - 1, chain - SIDE + 1 + me, 0)
    late = me > chain - SIDE
    relay = jnp.logical_or(late, first)
    target = jnp.where(first, SIDE, jnp.where(late, me - (chain - SIDE), me))

    def to_next(src, dst, send, recv):
        return pltpu.make_async_remote_copy(
            src_ref=src, dst_ref=dst, send_sem=send, recv_sem=recv,
            device_id={"layer": nxt}, device_id_type=MESH)

    def weight_copy(layer):
        return pltpu.make_async_copy(weights.at[layer], w.at[layer], w_sem.at[layer])

    def pair(ref, p):
        return ref.at[pl.ds(p * PAIR, PAIR)]

    def own_copy(p):
        return pltpu.make_async_copy(pair(warm, p), pair(own, p), own_sem.at[p])

    def input_copy(p):
        return pltpu.make_async_copy(pair(inputs, p), pair(start, p), start_recv.at[p])

    def warm_send(p):
        return to_next(pair(warm, p), pair(start, p), start_send.at[p], start_recv.at[p])

    def warm_aside(p):
        return pltpu.make_async_remote_copy(
            src_ref=pair(warm, p), dst_ref=pair(hold, p), send_sem=start_send.at[p],
            recv_sem=hold_recv.at[p], device_id={"layer": aside}, device_id_type=MESH)

    def warm_back(p):
        return pltpu.make_async_remote_copy(
            src_ref=pair(hold, p), dst_ref=pair(start, p), send_sem=hold_send.at[p],
            recv_sem=start_recv.at[p], device_id={"layer": target}, device_id_type=MESH)

    def slab(ref, j, h):
        return ref.at[j, pl.ds(h * (blocks // CUT), blocks // CUT)]

    def c1_copy(j, h, src=e1):
        at = j * CUT + h
        return to_next(slab(src, j, h), slab(c1, j, h), c1_send.at[at], c1_recv.at[at])

    def c2_copy(j, h):
        at = j * CUT + h
        return to_next(slab(e2, j, h), slab(c2, j, h), c2_send.at[at], c2_recv.at[at])

    def halves(do):
        for h in range(CUT):
            do(h)

    def part_copy():
        return to_next(part, before, part_send, part_recv)

    def peer_copy(hop):
        return pltpu.make_async_remote_copy(
            src_ref=part, dst_ref=around.at[hop - 1], send_sem=peer_send.at[hop - 1],
            recv_sem=peer_recv.at[hop - 1],
            device_id={"batch": lax.rem(mine + hop, peers)}, device_id_type=MESH)

    def total_copy(layer):
        return pltpu.make_async_remote_copy(
            src_ref=part, dst_ref=total, send_sem=total_send.at[layer], recv_sem=total_recv,
            device_id={"layer": layer}, device_id_type=MESH)

    def out_copy(j, buf):
        return pltpu.make_async_copy(buf.at[j], out.at[j], out_sem.at[j])

    def each(count, do):
        def body(j, carry):
            do(j)
            return carry
        lax.fori_loop(0, count, body, 0)

    def fetch(lo, hi):
        @pl.when(first)
        def _():
            each(hi - lo, lambda p: input_copy(p + lo).start())

        each(hi - lo, lambda p: own_copy(p + lo).start())

    weight_copy(0).start()
    fetch(0, DIRECT)
    for layer in range(1, layers):
        weight_copy(layer).start()
    fetch(DIRECT, pairs)

    barrier = pltpu.get_barrier_semaphore()

    def greet(**device):
        pl.semaphore_signal(barrier, inc=1, device_id=device, device_id_type=MESH)

    @pl.when(jnp.logical_not(first))
    def _():
        greet(layer=prv)

    @pl.when(jnp.logical_not(last))
    def _():
        greet(layer=chain - 1)

    @pl.when(last)
    def _():
        for hop in range(1, peers):
            greet(batch=lax.rem(mine + hop, peers))

    @pl.when(relay)
    def _():
        greet(layer=jnp.where(first, SIDE - 1, target - 1))

    @pl.when(jnp.logical_and(me >= 1, me <= SIDE))
    def _():
        greet(layer=jnp.where(me == SIDE, 0, me + chain - SIDE))

    def one(flag):
        return jnp.where(flag, 1, 0)

    pl.semaphore_wait(barrier, one(sender) + one(relay)
                      + jnp.where(last, chain - 1 + peers - 1, 1))

    @pl.when(jnp.logical_and(me < chain - SIDE, jnp.logical_not(sender)))
    def _():
        each(pairs, lambda p: warm_send(p).start())

    @pl.when(sender)
    def _():
        each(DIRECT, lambda p: warm_send(p).start())
        each(pairs - DIRECT, lambda p: warm_aside(p + DIRECT).start())

    def pass_on(p):
        warm_aside(p).wait_recv()
        warm_back(p).start()

    @pl.when(late)
    def _():
        each(pairs - DIRECT, lambda p: pass_on(p + DIRECT))

    @pl.when(jnp.logical_and(late, jnp.logical_not(last)))
    def _():
        each(pairs, lambda p: warm_send(p).start())

    acc[...] = jnp.zeros_like(acc)

    def layer_of(layer, src, epilogue, lo=0, hi=blocks, unroll=True):
        def body(c, carry):
            taken = [src[pat[layer, k, c]] for k in range(picks)]
            pre = jnp.dot(jnp.concatenate(taken, axis=1), w[layer, c],
                          preferred_element_type=jnp.float32)
            epilogue(c, jnp.tanh(pre + bias[layer:layer + 1, pl.ds(c * BLOCK, BLOCK)]))
            return carry
        lax.fori_loop(lo, hi, body, 0, unroll=unroll)

    def fold(x):
        return jnp.sum(x.reshape(x.shape[0] // 8, 8, BLOCK), axis=0)

    def relax_first(q):
        for i in range(QUAD // PAIR):
            p = q * (QUAD // PAIR) + i

            @pl.when(first)
            def _():
                input_copy(p).wait()

            @pl.when(jnp.logical_not(first))
            def _():
                warm_send(p).wait_recv()

            own_copy(p).wait()
        x = [start[q * QUAD + i].astype(jnp.float32) for i in range(QUAD)]
        ya[...] = jnp.concatenate(x, axis=1).astype(jnp.bfloat16)
        for i in range(QUAD):
            ref[:, i * ROWS:(i + 1) * ROWS] = own[q * QUAD + i].astype(jnp.float32)

        @pl.when(q == 0)
        def _():
            weight_copy(0).wait()

        def entry(c, t):
            x = ya[c].astype(jnp.float32)
            gc[c] = x + factor * t
            yb[c] = (x + STEP * t).astype(jnp.bfloat16)
        layer_of(0, ya, entry, unroll=16)

    def sweeps(q):
        def chunk(i, carry):
            @pl.when(jnp.logical_and(q > 0, jnp.logical_not(second)))
            def _():
                sweep_second((q - 1) * QUAD + i)

            @pl.when(q < quads)
            def _():
                sweep_first(q * QUAD + i, i)
            return carry
        lax.fori_loop(0, QUAD, chunk, 0)
        yb[...] = comb[...].astype(jnp.bfloat16)

    def sweep_first(j, i):
        halves(lambda h: c1_copy(j, h).wait_recv())
        xs[...] = c1[j]
        at_rows = pl.ds(pl.multiple_of(i * ROWS, ROWS), ROWS)

        def epilogue(c, t):
            x = xs[c].astype(jnp.float32)
            coarse = x + factor * t
            end = (coarse + tau[j, c]).astype(jnp.bfloat16)
            e1[j, c] = end
            gc[c, at_rows] = coarse
            ref[c, at_rows] = end.astype(jnp.float32)
            comb[c, at_rows] = x + STEP * t

        def part_of(h):
            layer_of(0, xs, epilogue, h * (blocks // CUT), (h + 1) * (blocks // CUT))

            @pl.when(jnp.logical_not(last))
            def _():
                c1_copy(j, h).start()
        halves(part_of)

    def fine(q, phase):
        src, dst = yb, ya
        for layer in range(1, layers):
            @pl.when(jnp.logical_and(q == 0, phase == 0))
            def _(layer=layer):
                weight_copy(layer).wait()

            def middle(c, t, src=src, dst=dst):
                dst[c] = (src[c].astype(jnp.float32) + STEP * t).astype(jnp.bfloat16)

            def final(c, t, src=src):
                g = (src[c].astype(jnp.float32) + STEP * t).astype(jnp.bfloat16).astype(jnp.float32)
                coarse = gc[c]
                correction = g - coarse
                joined = (coarse + correction).astype(jnp.bfloat16)
                for i in range(QUAD):
                    j = q * QUAD + i
                    at_rows = slice(i * ROWS, (i + 1) * ROWS)
                    tau[j, c] = correction[at_rows]
                    e2[j, c] = joined[at_rows]
                off = g - ref[c]
                acc[phase] += fold(off * off)
                off = g - joined.astype(jnp.float32)
                acc[2] += fold(off * off)
            layer_of(layer, src, middle if layer < layers - 1 else final)
            src, dst = dst, src

    def sweep_second(j):
        halves(lambda h: c2_copy(j, h).wait_recv())
        xs[...] = c2[j]

        def epilogue(c, t):
            x = xs[c].astype(jnp.float32)
            e2[j, c] = (x + factor * t + tau[j, c]).astype(jnp.bfloat16)

        def part_of(h):
            layer_of(0, xs, epilogue, h * (blocks // CUT), (h + 1) * (blocks // CUT))

            @pl.when(jnp.logical_not(last))
            def _():
                c2_copy(j, h).start()
        halves(part_of)
        out_copy(j, e2).start()

        @pl.when(jnp.logical_and(last, j == chunks - 3))
        def _():
            spread_total()

    def gather_part():
        part[0] = acc[0]
        part[1] = jnp.where(first, acc[2], acc[1])

        @pl.when(jnp.logical_not(first))
        def _():
            part_copy().wait_recv()
            part[...] += before[...]

        @pl.when(jnp.logical_not(last))
        def _():
            part_copy().start()

        @pl.when(last)
        def _():
            for hop in range(1, peers):
                peer_copy(hop).start()

    def spread_total():
        for hop in range(1, peers):
            peer_copy(hop).wait()
        part[...] += jnp.sum(around[...], axis=0)
        for layer in range(chain - 1):
            total_copy(layer).start()
        total[...] = part[...]

    lead = jnp.where(first, 0, jnp.clip(2 * (me - SIDE) + 1, 0, quads))

    def step(s, carry):
        def phase_of(phase, carry):
            q = jnp.where(phase == 0, s, s - lead)
            run = jnp.where(phase == 0, s < quads,
                            jnp.logical_and(q >= 0, jnp.logical_not(first)))

            @pl.when(run)
            def _():
                @pl.when(phase == 0)
                def _():
                    relax_first(q)

                @pl.when(phase == 1)
                def _():
                    sweeps(q)

                @pl.when(q < quads)
                def _():
                    fine(q, phase)
            return carry
        lax.fori_loop(0, ITERS, phase_of, 0)
        q = s - lead

        @pl.when(q == quads - 1)
        def _():
            gather_part()

        @pl.when(first)
        def _():
            for i in range(QUAD):
                halves(lambda h: c1_copy(q * QUAD + i, h, e2).start())
                out_copy(q * QUAD + i, e2).start()
            for i in range(QUAD // PAIR):
                p = q * (QUAD // PAIR) + i

                @pl.when(p >= DIRECT)
                def _():
                    pass_on(p)

        @pl.when(second)
        def _():
            for i in range(QUAD):
                halves(lambda h: c2_copy(q * QUAD + i, h).start())
                out_copy(q * QUAD + i, e2).start()

        @pl.when(jnp.logical_and(s == quads - 1, me == chain - SIDE))
        def _():
            each(pairs, lambda p: warm_send(p).start())

        return carry

    lax.fori_loop(0, quads + lead + jnp.where(me >= 2, 1, 0), step, 0)

    @pl.when(last)
    def _():
        for layer in range(chain - 1):
            total_copy(layer).wait_send()

    @pl.when(jnp.logical_not(last))
    def _():
        part_copy().wait_send()
        total_copy(0).wait_recv()
        each(pairs, lambda p: warm_send(p).wait_send())
        each(chunks, lambda j: halves(lambda h: c1_copy(j, h).wait_send()))

    @pl.when(jnp.logical_and(jnp.logical_not(last), jnp.logical_not(first)))
    def _():
        each(chunks, lambda j: halves(lambda h: c2_copy(j, h).wait_send()))

    @pl.when(relay)
    def _():
        each(pairs - DIRECT, lambda p: warm_back(p + DIRECT).wait_send())

    each(chunks, lambda j: out_copy(j, e2).wait())
    for i in range(ITERS):
        norms[i] = jnp.sum(total[i])


def on_device(inputs, warm_states, weights, pattern, bias):
    chain = lax.axis_size("layer")
    rows, width = inputs.shape
    layers, blocks, picks, size, _ = weights.shape
    chunks = rows // ROWS
    count = float(chain * lax.axis_size("batch") * rows * width)

    def pieces(x):
        return x.reshape(chunks, ROWS, blocks, size).transpose(0, 2, 1, 3)

    any_ = pl.BlockSpec(memory_space=pl.ANY)
    vmem = pl.BlockSpec(memory_space=pltpu.VMEM)
    piece = (chunks, blocks, ROWS, size)
    dma = pltpu.SemaphoreType.DMA
    peers = lax.axis_size("batch")
    ends, norms = pl.pallas_call(
        functools.partial(kernel, chain, peers),
        out_shape=(
            jax.ShapeDtypeStruct(piece, jnp.bfloat16),
            jax.ShapeDtypeStruct((ITERS,), jnp.float32),
        ),
        in_specs=[pl.BlockSpec(memory_space=pltpu.SMEM), any_, any_, any_, vmem],
        out_specs=(any_, pl.BlockSpec(memory_space=pltpu.SMEM)),
        scratch_shapes=[
            pltpu.VMEM((layers, blocks, picks * size, size), jnp.bfloat16),
            *[pltpu.VMEM(piece, jnp.bfloat16)] * 7,
            pltpu.VMEM(piece, jnp.float32),
            pltpu.VMEM((blocks, ROWS, size), jnp.bfloat16),
            *[pltpu.VMEM((blocks, QUAD * ROWS, size), jnp.bfloat16)] * 2,
            *[pltpu.VMEM((blocks, QUAD * ROWS, size), jnp.float32)] * 3,
            pltpu.VMEM((3, 8, BLOCK), jnp.float32),
            *[pltpu.VMEM((ITERS, 8, BLOCK), jnp.float32)] * 2,
            pltpu.VMEM((peers - 1, ITERS, 8, BLOCK), jnp.float32),
            pltpu.VMEM((ITERS, 8, BLOCK), jnp.float32),
            dma((layers,)),
            *[dma((chunks // PAIR,))] * 5,
            *[dma((chunks * CUT,))] * 4,
            dma((chunks,)),
            dma, dma, dma((peers - 1,)), dma((peers - 1,)), dma((chain - 1,)), dma,
        ],
        compiler_params=pltpu.CompilerParams(
            collective_id=0, has_side_effects=True, vmem_limit_bytes=60 << 20),
    )(
        pattern.transpose(0, 2, 1),
        pieces(inputs),
        pieces(warm_states),
        weights.reshape(layers, blocks, picks * size, size),
        bias,
    )
    ends = ends.transpose(0, 2, 1, 3).reshape(1, rows, width)
    return ends, jnp.sqrt(norms / count)


def solution(mesh):
    in_specs = (
        P("batch", None),
        P("layer", "batch", None),
        P("layer", None, None, None, None),
        P("layer", None, None),
        P("layer", None),
    )
    return jax.shard_map(
        on_device, mesh=mesh, in_specs=in_specs,
        out_specs=(P("layer", "batch", None), P()), check_vma=False)
```

```python
import functools

import jax
import jax.numpy as jnp
from jax import lax
from jax.experimental import pallas as pl
from jax.experimental.pallas import tpu as pltpu
from jax.sharding import PartitionSpec as P

MESH = pl.DeviceIdType.MESH
STEP = 0.25
ITERS = 2
ROWS = 8
PAIR = 2
QUAD = 4
CUT = 2
DIRECT = 2
SPREAD = 8
SIDE = 4
BLOCK = 128


def kernel(chain, peers, pat, inputs, warm, weights, bias, out, norms, w, start, own, c1, c2, e1, e2, hold, tau,
           xs, ya, yb, gy, za, zb, gc, ref, comb, acc, part, before, around, total, w_sem, own_sem, start_send, start_recv,
           hold_send, hold_recv, c1_send, c1_recv,
           c2_send, c2_recv, out_sem,
           part_send, part_recv, peer_send, peer_recv, total_send, total_recv):
    me = lax.axis_index("layer")
    mine = lax.axis_index("batch")
    nxt, prv = lax.rem(me + 1, chain), lax.rem(me + chain - 1, chain)
    layers, blocks, picks = weights.shape[0], weights.shape[1], 4
    factor = layers * STEP
    chunks = inputs.shape[0]
    pairs = chunks // PAIR
    first, second, last = me == 0, me == 1, me == chain - 1
    quads = chunks // QUAD
    sender = me < SIDE
    aside = jnp.where(me < SIDE - 1, chain - SIDE + 1 + me, 0)
    late = me > chain - SIDE
    relay = jnp.logical_or(late, first)
    target = jnp.where(first, SIDE, jnp.where(late, me - (chain - SIDE), me))

    def to_next(src, dst, send, recv):
        return pltpu.make_async_remote_copy(
            src_ref=src, dst_ref=dst, send_sem=send, recv_sem=recv,
            device_id={"layer": nxt}, device_id_type=MESH)

    def weight_copy(layer):
        return pltpu.make_async_copy(weights.at[layer], w.at[layer], w_sem.at[layer])

    def pair(ref, p):
        return ref.at[pl.ds(p * PAIR, PAIR)]

    def own_copy(p):
        return pltpu.make_async_copy(pair(warm, p), pair(own, p), own_sem.at[p])

    def input_copy(p):
        return pltpu.make_async_copy(pair(inputs, p), pair(start, p), start_recv.at[p])

    def warm_send(p):
        return to_next(pair(warm, p), pair(start, p), start_send.at[p], start_recv.at[p])

    def warm_aside(p):
        return pltpu.make_async_remote_copy(
            src_ref=pair(warm, p), dst_ref=pair(hold, p), send_sem=start_send.at[p],
            recv_sem=hold_recv.at[p], device_id={"layer": aside}, device_id_type=MESH)

    def warm_back(p):
        return pltpu.make_async_remote_copy(
            src_ref=pair(hold, p), dst_ref=pair(start, p), send_sem=hold_send.at[p],
            recv_sem=start_recv.at[p], device_id={"layer": target}, device_id_type=MESH)

    def slab(ref, j, h):
        return ref.at[j, pl.ds(h * (blocks // CUT), blocks // CUT)]

    def c1_copy(j, h, src=e1):
        at = j * CUT + h
        return to_next(slab(src, j, h), slab(c1, j, h), c1_send.at[at], c1_recv.at[at])

    def c2_copy(j, h):
        at = j * CUT + h
        return to_next(slab(e2, j, h), slab(c2, j, h), c2_send.at[at], c2_recv.at[at])

    def halves(do):
        for h in range(CUT):
            do(h)

    def part_copy():
        return to_next(part, before, part_send, part_recv)

    def peer_copy(hop):
        return pltpu.make_async_remote_copy(
            src_ref=part, dst_ref=around.at[hop - 1], send_sem=peer_send.at[hop - 1],
            recv_sem=peer_recv.at[hop - 1],
            device_id={"batch": lax.rem(mine + hop, peers)}, device_id_type=MESH)

    def total_copy(layer):
        return pltpu.make_async_remote_copy(
            src_ref=part, dst_ref=total, send_sem=total_send.at[layer], recv_sem=total_recv,
            device_id={"layer": layer}, device_id_type=MESH)

    def out_copy(j, buf):
        return pltpu.make_async_copy(buf.at[j], out.at[j], out_sem.at[j])

    def each(count, do):
        def body(j, carry):
            do(j)
            return carry
        lax.fori_loop(0, count, body, 0)

    def fetch(lo, hi):
        @pl.when(first)
        def _():
            each(hi - lo, lambda p: input_copy(p + lo).start())

        each(hi - lo, lambda p: own_copy(p + lo).start())

    weight_copy(0).start()
    fetch(0, DIRECT)
    for layer in range(1, layers):
        weight_copy(layer).start()
    fetch(DIRECT, pairs)

    barrier = pltpu.get_barrier_semaphore()

    def greet(**device):
        pl.semaphore_signal(barrier, inc=1, device_id=device, device_id_type=MESH)

    @pl.when(jnp.logical_not(first))
    def _():
        greet(layer=prv)

    @pl.when(jnp.logical_not(last))
    def _():
        greet(layer=chain - 1)

    @pl.when(last)
    def _():
        for hop in range(1, peers):
            greet(batch=lax.rem(mine + hop, peers))

    @pl.when(relay)
    def _():
        greet(layer=jnp.where(first, SIDE - 1, target - 1))

    @pl.when(jnp.logical_and(me >= 1, me <= SIDE))
    def _():
        greet(layer=jnp.where(me == SIDE, 0, me + chain - SIDE))

    def one(flag):
        return jnp.where(flag, 1, 0)

    pl.semaphore_wait(barrier, one(sender) + one(relay)
                      + jnp.where(last, chain - 1 + peers - 1, 1))

    @pl.when(jnp.logical_and(me < chain - SIDE, jnp.logical_not(sender)))
    def _():
        each(pairs, lambda p: warm_send(p).start())

    @pl.when(sender)
    def _():
        each(DIRECT, lambda p: warm_send(p).start())
        each(pairs - DIRECT, lambda p: warm_aside(p + DIRECT).start())

    def pass_on(p):
        warm_aside(p).wait_recv()
        warm_back(p).start()

    @pl.when(late)
    def _():
        each(pairs - DIRECT, lambda p: pass_on(p + DIRECT))

    @pl.when(jnp.logical_and(late, jnp.logical_not(last)))
    def _():
        each(pairs, lambda p: warm_send(p).start())

    acc[...] = jnp.zeros_like(acc)

    def layer_of(layer, src, epilogue, lo=0, hi=blocks, unroll=True):
        def body(c, carry):
            taken = [src[pat[layer, k, c]] for k in range(picks)]
            pre = jnp.dot(jnp.concatenate(taken, axis=1), w[layer, c],
                          preferred_element_type=jnp.float32)
            epilogue(c, jnp.tanh(pre + bias[layer:layer + 1, pl.ds(c * BLOCK, BLOCK)]))
            return carry
        lax.fori_loop(lo, hi, body, 0, unroll=unroll)

    def fold(x):
        return jnp.sum(x.reshape(x.shape[0] // 8, 8, BLOCK), axis=0)

    def relax_first(q):
        for i in range(QUAD // PAIR):
            p = q * (QUAD // PAIR) + i

            @pl.when(first)
            def _():
                input_copy(p).wait()

            @pl.when(jnp.logical_not(first))
            def _():
                warm_send(p).wait_recv()

            own_copy(p).wait()
        x = [start[q * QUAD + i].astype(jnp.float32) for i in range(QUAD)]
        ya[...] = jnp.concatenate(x, axis=1).astype(jnp.bfloat16)
        @pl.when(q == 0)
        def _():
            weight_copy(0).wait()

        def entry(c, t):
            x = ya[c].astype(jnp.float32)
            gy[c] = x + factor * t
            yb[c] = (x + STEP * t).astype(jnp.bfloat16)
        layer_of(0, ya, entry, unroll=16)

        def off_of(g, c, i):
            return g - own[q * QUAD + i, c].astype(jnp.float32)
        fine(yb, ya, gy, off_of, q * QUAD, QUAD, 0, q == 0)

    def sweep_ahead(q):
        def chunk(i, carry):
            sweep_first(q * QUAD + i)
            return carry
        lax.fori_loop(0, QUAD, chunk, 0)

    def relax_second():
        zb[...] = comb[...].astype(jnp.bfloat16)

        def off_of(g, c, i):
            return g - ref[c, i * ROWS:(i + 1) * ROWS]
        fine(zb, za, gc, off_of, 0, chunks, 1)

    def sweep_first(j):
        halves(lambda h: c1_copy(j, h).wait_recv())
        xs[...] = c1[j]
        at_rows = pl.ds(pl.multiple_of(j * ROWS, ROWS), ROWS)

        def epilogue(c, t):
            x = xs[c].astype(jnp.float32)
            coarse = x + factor * t
            end = (coarse + tau[j, c]).astype(jnp.bfloat16)
            e1[j, c] = end
            gc[c, at_rows] = coarse
            ref[c, at_rows] = end.astype(jnp.float32)
            comb[c, at_rows] = x + STEP * t

        def part_of(h):
            layer_of(0, xs, epilogue, h * (blocks // CUT), (h + 1) * (blocks // CUT))

            @pl.when(jnp.logical_not(last))
            def _():
                c1_copy(j, h).start()
        halves(part_of)

    def fine(src, dst, base, off_of, start_at, count, phase, fresh=None):
        for layer in range(1, layers):
            if fresh is not None:
                @pl.when(fresh)
                def _(layer=layer):
                    weight_copy(layer).wait()

            def middle(c, t, src=src, dst=dst):
                dst[c] = (src[c].astype(jnp.float32) + STEP * t).astype(jnp.bfloat16)

            def final(c, t, src=src):
                g = (src[c].astype(jnp.float32) + STEP * t).astype(jnp.bfloat16).astype(jnp.float32)
                coarse = base[c]
                correction = g - coarse
                joined = (coarse + correction).astype(jnp.bfloat16)
                total_off = jnp.zeros((ROWS, BLOCK), jnp.float32)
                for i in range(count):
                    at_rows = slice(i * ROWS, (i + 1) * ROWS)
                    tau[start_at + i, c] = correction[at_rows]
                    e2[start_at + i, c] = joined[at_rows]
                    off = off_of(g[at_rows], c, i)
                    total_off += off * off
                acc[phase] += total_off
                if phase == 0:
                    off = g - joined.astype(jnp.float32)
                    acc[2] += fold(off * off)
            layer_of(layer, src, middle if layer < layers - 1 else final)
            src, dst = dst, src

    def sweep_second(j):
        halves(lambda h: c2_copy(j, h).wait_recv())
        xs[...] = c2[j]

        def epilogue(c, t):
            x = xs[c].astype(jnp.float32)
            e2[j, c] = (x + factor * t + tau[j, c]).astype(jnp.bfloat16)

        def part_of(h):
            layer_of(0, xs, epilogue, h * (blocks // CUT), (h + 1) * (blocks // CUT))

            @pl.when(jnp.logical_not(last))
            def _():
                c2_copy(j, h).start()
        halves(part_of)
        out_copy(j, e2).start()

        @pl.when(j == 1)
        def _():
            gather_part()

        @pl.when(jnp.logical_and(last, j == SPREAD))
        def _():
            spread_total()

    def gather_part():
        part[0] = acc[0]
        part[1] = jnp.where(first, acc[2], acc[1])

        @pl.when(jnp.logical_not(first))
        def _():
            part_copy().wait_recv()
            part[...] += before[...]

        @pl.when(jnp.logical_not(last))
        def _():
            part_copy().start()

        @pl.when(last)
        def _():
            for hop in range(1, peers):
                peer_copy(hop).start()

    def spread_total():
        for hop in range(1, peers):
            peer_copy(hop).wait()
        part[...] += jnp.sum(around[...], axis=0)
        for layer in range(chain - 1):
            total_copy(layer).start()
        total[...] = part[...]

    lead = jnp.where(first, 0, jnp.clip(2 * (me - SIDE) + 1, 0, quads))

    def step(s, carry):
        q = s - lead

        @pl.when(s < quads)
        def _():
            relax_first(s)

        @pl.when(first)
        def _():
            for i in range(QUAD):
                halves(lambda h: c1_copy(q * QUAD + i, h, e2).start())
                out_copy(q * QUAD + i, e2).start()
            for i in range(QUAD // PAIR):
                p = q * (QUAD // PAIR) + i

                @pl.when(p >= DIRECT)
                def _():
                    pass_on(p)

        @pl.when(jnp.logical_and(s == quads - 1, me == chain - SIDE))
        def _():
            each(pairs, lambda p: warm_send(p).start())

        @pl.when(jnp.logical_and(q >= 0, jnp.logical_not(first)))
        def _():
            sweep_ahead(q)

        return carry

    lax.fori_loop(0, quads + lead, step, 0)

    @pl.when(jnp.logical_not(first))
    def _():
        relax_second()

    @pl.when(me < 2)
    def _():
        gather_part()

    @pl.when(second)
    def _():
        def send(j):
            halves(lambda h: c2_copy(j, h).start())
            out_copy(j, e2).start()
        each(chunks, send)

    @pl.when(me >= 2)
    def _():
        each(chunks, sweep_second)

    @pl.when(last)
    def _():
        for layer in range(chain - 1):
            total_copy(layer).wait_send()

    @pl.when(jnp.logical_not(last))
    def _():
        part_copy().wait_send()
        total_copy(0).wait_recv()
        each(pairs, lambda p: warm_send(p).wait_send())
        each(chunks, lambda j: halves(lambda h: c1_copy(j, h).wait_send()))

    @pl.when(jnp.logical_and(jnp.logical_not(last), jnp.logical_not(first)))
    def _():
        each(chunks, lambda j: halves(lambda h: c2_copy(j, h).wait_send()))

    @pl.when(relay)
    def _():
        each(pairs - DIRECT, lambda p: warm_back(p + DIRECT).wait_send())

    each(chunks, lambda j: out_copy(j, e2).wait())
    for i in range(ITERS):
        norms[i] = jnp.sum(total[i])


def on_device(inputs, warm_states, weights, pattern, bias):
    chain = lax.axis_size("layer")
    rows, width = inputs.shape
    layers, blocks, picks, size, _ = weights.shape
    chunks = rows // ROWS
    count = float(chain * lax.axis_size("batch") * rows * width)

    def pieces(x):
        return x.reshape(chunks, ROWS, blocks, size).transpose(0, 2, 1, 3)

    any_ = pl.BlockSpec(memory_space=pl.ANY)
    vmem = pl.BlockSpec(memory_space=pltpu.VMEM)
    piece = (chunks, blocks, ROWS, size)
    dma = pltpu.SemaphoreType.DMA
    peers = lax.axis_size("batch")
    ends, norms = pl.pallas_call(
        functools.partial(kernel, chain, peers),
        out_shape=(
            jax.ShapeDtypeStruct(piece, jnp.bfloat16),
            jax.ShapeDtypeStruct((ITERS,), jnp.float32),
        ),
        in_specs=[pl.BlockSpec(memory_space=pltpu.SMEM), any_, any_, any_, vmem],
        out_specs=(any_, pl.BlockSpec(memory_space=pltpu.SMEM)),
        scratch_shapes=[
            pltpu.VMEM((layers, blocks, picks * size, size), jnp.bfloat16),
            *[pltpu.VMEM(piece, jnp.bfloat16)] * 7,
            pltpu.VMEM(piece, jnp.float32),
            pltpu.VMEM((blocks, ROWS, size), jnp.bfloat16),
            *[pltpu.VMEM((blocks, QUAD * ROWS, size), jnp.bfloat16)] * 2,
            pltpu.VMEM((blocks, QUAD * ROWS, size), jnp.float32),
            *[pltpu.VMEM((blocks, rows, size), jnp.bfloat16)] * 2,
            *[pltpu.VMEM((blocks, rows, size), jnp.float32)] * 3,
            pltpu.VMEM((3, 8, BLOCK), jnp.float32),
            *[pltpu.VMEM((ITERS, 8, BLOCK), jnp.float32)] * 2,
            pltpu.VMEM((peers - 1, ITERS, 8, BLOCK), jnp.float32),
            pltpu.VMEM((ITERS, 8, BLOCK), jnp.float32),
            dma((layers,)),
            *[dma((chunks // PAIR,))] * 5,
            *[dma((chunks * CUT,))] * 4,
            dma((chunks,)),
            dma, dma, dma((peers - 1,)), dma((peers - 1,)), dma((chain - 1,)), dma,
        ],
        compiler_params=pltpu.CompilerParams(
            collective_id=0, has_side_effects=True, vmem_limit_bytes=60 << 20),
    )(
        pattern.transpose(0, 2, 1),
        pieces(inputs),
        pieces(warm_states),
        weights.reshape(layers, blocks, picks * size, size),
        bias,
    )
    ends = ends.transpose(0, 2, 1, 3).reshape(1, rows, width)
    return ends, jnp.sqrt(norms / count)


def solution(mesh):
    in_specs = (
        P("batch", None),
        P("layer", "batch", None),
        P("layer", None, None, None, None),
        P("layer", None, None),
        P("layer", None),
    )
    return jax.shard_map(
        on_device, mesh=mesh, in_specs=in_specs,
        out_specs=(P("layer", "batch", None), P()), check_vma=False)
```

```python
import functools

import jax
import jax.numpy as jnp
from jax import lax
from jax.experimental import pallas as pl
from jax.experimental.pallas import tpu as pltpu
from jax.sharding import PartitionSpec as P

MESH = pl.DeviceIdType.MESH
STEP = 0.25
ITERS = 2
ROWS = 8
PAIR = 2
QUAD = 4
CUT = 2
DIRECT = 2
SPREAD = 6
SIDE = 4
BLOCK = 128


def kernel(chain, peers, pat, inputs, warm, weights, bias, out, norms, w, start, own, c1, c2, e1, e2, hold, tau,
           xs, ya, yb, gy, za, zb, gc, ref, comb, acc, part, before, around, total, w_sem, own_sem, start_send, start_recv,
           hold_send, hold_recv, c1_send, c1_recv,
           c2_send, c2_recv, out_sem,
           part_send, part_recv, peer_send, peer_recv, total_send, total_recv):
    me = lax.axis_index("layer")
    mine = lax.axis_index("batch")
    nxt, prv = lax.rem(me + 1, chain), lax.rem(me + chain - 1, chain)
    layers, blocks, picks = weights.shape[0], weights.shape[1], 4
    factor = layers * STEP
    chunks = inputs.shape[0]
    pairs = chunks // PAIR
    first, second, last = me == 0, me == 1, me == chain - 1
    quads = chunks // QUAD
    sender = me < SIDE
    aside = jnp.where(me < SIDE - 1, chain - SIDE + 1 + me, 0)
    late = me > chain - SIDE
    relay = jnp.logical_or(late, first)
    target = jnp.where(first, SIDE, jnp.where(late, me - (chain - SIDE), me))

    def to_next(src, dst, send, recv):
        return pltpu.make_async_remote_copy(
            src_ref=src, dst_ref=dst, send_sem=send, recv_sem=recv,
            device_id={"layer": nxt}, device_id_type=MESH)

    def weight_copy(layer):
        return pltpu.make_async_copy(weights.at[layer], w.at[layer], w_sem.at[layer])

    def pair(ref, p):
        return ref.at[pl.ds(p * PAIR, PAIR)]

    def own_copy(p):
        return pltpu.make_async_copy(pair(warm, p), pair(own, p), own_sem.at[p])

    def input_copy(p):
        return pltpu.make_async_copy(pair(inputs, p), pair(start, p), start_recv.at[p])

    def warm_send(p):
        return to_next(pair(warm, p), pair(start, p), start_send.at[p], start_recv.at[p])

    def warm_aside(p):
        return pltpu.make_async_remote_copy(
            src_ref=pair(warm, p), dst_ref=pair(hold, p), send_sem=start_send.at[p],
            recv_sem=hold_recv.at[p], device_id={"layer": aside}, device_id_type=MESH)

    def warm_back(p):
        return pltpu.make_async_remote_copy(
            src_ref=pair(hold, p), dst_ref=pair(start, p), send_sem=hold_send.at[p],
            recv_sem=start_recv.at[p], device_id={"layer": target}, device_id_type=MESH)

    def slab(ref, j, h):
        return ref.at[j, pl.ds(h * (blocks // CUT), blocks // CUT)]

    def c1_copy(j, h, src=e1):
        at = j * CUT + h
        return to_next(slab(src, j, h), slab(c1, j, h), c1_send.at[at], c1_recv.at[at])

    def c2_copy(j, h):
        at = j * CUT + h
        return to_next(slab(e2, j, h), slab(c2, j, h), c2_send.at[at], c2_recv.at[at])

    def halves(do):
        for h in range(CUT):
            do(h)

    def part_copy():
        return to_next(part, before, part_send, part_recv)

    def peer_copy(hop):
        return pltpu.make_async_remote_copy(
            src_ref=part, dst_ref=around.at[hop - 1], send_sem=peer_send.at[hop - 1],
            recv_sem=peer_recv.at[hop - 1],
            device_id={"batch": lax.rem(mine + hop, peers)}, device_id_type=MESH)

    def total_copy(layer):
        return pltpu.make_async_remote_copy(
            src_ref=part, dst_ref=total, send_sem=total_send.at[layer], recv_sem=total_recv,
            device_id={"layer": layer}, device_id_type=MESH)

    def out_copy(j, buf):
        return pltpu.make_async_copy(buf.at[j], out.at[j], out_sem.at[j])

    def each(count, do):
        def body(j, carry):
            do(j)
            return carry
        lax.fori_loop(0, count, body, 0)

    def fetch(lo, hi):
        @pl.when(first)
        def _():
            each(hi - lo, lambda p: input_copy(p + lo).start())

        each(hi - lo, lambda p: own_copy(p + lo).start())

    weight_copy(0).start()
    fetch(0, DIRECT)
    for layer in range(1, layers):
        weight_copy(layer).start()
    fetch(DIRECT, pairs)

    barrier = pltpu.get_barrier_semaphore()

    def greet(**device):
        pl.semaphore_signal(barrier, inc=1, device_id=device, device_id_type=MESH)

    @pl.when(jnp.logical_not(first))
    def _():
        greet(layer=prv)

    @pl.when(jnp.logical_not(last))
    def _():
        greet(layer=chain - 1)

    @pl.when(last)
    def _():
        for hop in range(1, peers):
            greet(batch=lax.rem(mine + hop, peers))

    @pl.when(relay)
    def _():
        greet(layer=jnp.where(first, SIDE - 1, target - 1))

    @pl.when(jnp.logical_and(me >= 1, me <= SIDE))
    def _():
        greet(layer=jnp.where(me == SIDE, 0, me + chain - SIDE))

    def one(flag):
        return jnp.where(flag, 1, 0)

    pl.semaphore_wait(barrier, one(sender) + one(relay)
                      + jnp.where(last, chain - 1 + peers - 1, 1))

    @pl.when(jnp.logical_and(me < chain - SIDE, jnp.logical_not(sender)))
    def _():
        each(pairs, lambda p: warm_send(p).start())

    @pl.when(sender)
    def _():
        each(DIRECT, lambda p: warm_send(p).start())
        each(pairs - DIRECT, lambda p: warm_aside(p + DIRECT).start())

    def pass_on(p):
        warm_aside(p).wait_recv()
        warm_back(p).start()

    @pl.when(late)
    def _():
        each(pairs - DIRECT, lambda p: pass_on(p + DIRECT))

    @pl.when(jnp.logical_and(late, jnp.logical_not(last)))
    def _():
        each(pairs, lambda p: warm_send(p).start())

    acc[...] = jnp.zeros_like(acc)

    def layer_of(layer, src, epilogue, lo=0, hi=blocks, unroll=True):
        def body(c, carry):
            taken = [src[pat[layer, k, c]] for k in range(picks)]
            pre = jnp.dot(jnp.concatenate(taken, axis=1), w[layer, c],
                          preferred_element_type=jnp.float32)
            epilogue(c, jnp.tanh(pre + bias[layer:layer + 1, pl.ds(c * BLOCK, BLOCK)]))
            return carry
        lax.fori_loop(lo, hi, body, 0, unroll=unroll)

    def fold(x):
        return jnp.sum(x.reshape(x.shape[0] // 8, 8, BLOCK), axis=0)

    def relax_first(q):
        for i in range(QUAD // PAIR):
            p = q * (QUAD // PAIR) + i

            @pl.when(first)
            def _():
                input_copy(p).wait()

            @pl.when(jnp.logical_not(first))
            def _():
                warm_send(p).wait_recv()

            own_copy(p).wait()
        x = [start[q * QUAD + i].astype(jnp.float32) for i in range(QUAD)]
        ya[...] = jnp.concatenate(x, axis=1).astype(jnp.bfloat16)
        @pl.when(q == 0)
        def _():
            weight_copy(0).wait()

        def entry(c, t):
            x = ya[c].astype(jnp.float32)
            gy[c] = x + factor * t
            yb[c] = (x + STEP * t).astype(jnp.bfloat16)
        layer_of(0, ya, entry, unroll=16)

        def off_of(g, c, i):
            return g - own[q * QUAD + i, c].astype(jnp.float32)
        fine(yb, ya, gy, off_of, q * QUAD, QUAD, 0, q == 0)

    def sweep_ahead(q):
        def chunk(i, carry):
            sweep_first(q * QUAD + i)
            return carry
        lax.fori_loop(0, QUAD, chunk, 0)

    def relax_second():
        zb[...] = comb[...].astype(jnp.bfloat16)

        def off_of(g, c, i):
            return g - ref[c, i * ROWS:(i + 1) * ROWS]
        fine(zb, za, gc, off_of, 0, chunks, 1)

    def sweep_first(j):
        halves(lambda h: c1_copy(j, h).wait_recv())
        xs[...] = c1[j]
        at_rows = pl.ds(pl.multiple_of(j * ROWS, ROWS), ROWS)

        def epilogue(c, t):
            x = xs[c].astype(jnp.float32)
            coarse = x + factor * t
            end = (coarse + tau[j, c]).astype(jnp.bfloat16)
            e1[j, c] = end
            gc[c, at_rows] = coarse
            ref[c, at_rows] = end.astype(jnp.float32)
            comb[c, at_rows] = x + STEP * t

        def part_of(h):
            layer_of(0, xs, epilogue, h * (blocks // CUT), (h + 1) * (blocks // CUT))

            @pl.when(jnp.logical_not(last))
            def _():
                c1_copy(j, h).start()
        halves(part_of)

    def fine(src, dst, base, off_of, start_at, count, phase, fresh=None):
        for layer in range(1, layers):
            if fresh is not None:
                @pl.when(fresh)
                def _(layer=layer):
                    weight_copy(layer).wait()

            def middle(c, t, src=src, dst=dst):
                dst[c] = (src[c].astype(jnp.float32) + STEP * t).astype(jnp.bfloat16)

            def final(c, t, src=src):
                g = (src[c].astype(jnp.float32) + STEP * t).astype(jnp.bfloat16).astype(jnp.float32)
                coarse = base[c]
                correction = g - coarse
                joined = (coarse + correction).astype(jnp.bfloat16)
                total_off = jnp.zeros((ROWS, BLOCK), jnp.float32)
                for i in range(count):
                    at_rows = slice(i * ROWS, (i + 1) * ROWS)
                    tau[start_at + i, c] = correction[at_rows]
                    e2[start_at + i, c] = joined[at_rows]
                    off = off_of(g[at_rows], c, i)
                    total_off += off * off
                acc[phase] += total_off
                if phase == 0:
                    off = g - joined.astype(jnp.float32)
                    acc[2] += fold(off * off)
            layer_of(layer, src, middle if layer < layers - 1 else final)
            src, dst = dst, src

    def sweep_second(j):
        halves(lambda h: c2_copy(j, h).wait_recv())
        xs[...] = c2[j]

        def epilogue(c, t):
            x = xs[c].astype(jnp.float32)
            e2[j, c] = (x + factor * t + tau[j, c]).astype(jnp.bfloat16)

        def part_of(h):
            layer_of(0, xs, epilogue, h * (blocks // CUT), (h + 1) * (blocks // CUT))

            @pl.when(jnp.logical_not(last))
            def _():
                c2_copy(j, h).start()
        halves(part_of)
        out_copy(j, e2).start()

        @pl.when(j == 1)
        def _():
            gather_part()

        @pl.when(jnp.logical_and(last, j == SPREAD))
        def _():
            spread_total()

    def gather_part():
        part[0] = acc[0]
        part[1] = jnp.where(first, acc[2], acc[1])

        @pl.when(jnp.logical_not(first))
        def _():
            part_copy().wait_recv()
            part[...] += before[...]

        @pl.when(jnp.logical_not(last))
        def _():
            part_copy().start()

        @pl.when(last)
        def _():
            for hop in range(1, peers):
                peer_copy(hop).start()

    def spread_total():
        for hop in range(1, peers):
            peer_copy(hop).wait()
        part[...] += jnp.sum(around[...], axis=0)
        for layer in range(chain - 1):
            total_copy(layer).start()
        total[...] = part[...]

    lead = jnp.where(first, 0, jnp.clip(2 * (me - SIDE) + 1, 0, quads))

    def step(s, carry):
        q = s - lead

        @pl.when(s < quads)
        def _():
            relax_first(s)

        @pl.when(first)
        def _():
            for i in range(QUAD):
                halves(lambda h: c1_copy(q * QUAD + i, h, e2).start())
                out_copy(q * QUAD + i, e2).start()
            for i in range(QUAD // PAIR):
                p = q * (QUAD // PAIR) + i

                @pl.when(p >= DIRECT)
                def _():
                    pass_on(p)

        @pl.when(jnp.logical_and(s == quads - 1, me == chain - SIDE))
        def _():
            each(pairs, lambda p: warm_send(p).start())

        @pl.when(jnp.logical_and(q >= 0, jnp.logical_not(first)))
        def _():
            sweep_ahead(q)

        return carry

    lax.fori_loop(0, quads + lead, step, 0)

    @pl.when(jnp.logical_not(first))
    def _():
        relax_second()

    @pl.when(me < 2)
    def _():
        gather_part()

    @pl.when(second)
    def _():
        def send(j):
            halves(lambda h: c2_copy(j, h).start())
            out_copy(j, e2).start()
        each(chunks, send)

    @pl.when(me >= 2)
    def _():
        each(chunks, sweep_second)

    @pl.when(last)
    def _():
        for layer in range(chain - 1):
            total_copy(layer).wait_send()

    @pl.when(jnp.logical_not(last))
    def _():
        part_copy().wait_send()
        total_copy(0).wait_recv()
        each(pairs, lambda p: warm_send(p).wait_send())
        each(chunks, lambda j: halves(lambda h: c1_copy(j, h).wait_send()))

    @pl.when(jnp.logical_and(jnp.logical_not(last), jnp.logical_not(first)))
    def _():
        each(chunks, lambda j: halves(lambda h: c2_copy(j, h).wait_send()))

    @pl.when(relay)
    def _():
        each(pairs - DIRECT, lambda p: warm_back(p + DIRECT).wait_send())

    each(chunks, lambda j: out_copy(j, e2).wait())
    for i in range(ITERS):
        norms[i] = jnp.sum(total[i])


def on_device(inputs, warm_states, weights, pattern, bias):
    chain = lax.axis_size("layer")
    rows, width = inputs.shape
    layers, blocks, picks, size, _ = weights.shape
    chunks = rows // ROWS
    count = float(chain * lax.axis_size("batch") * rows * width)

    def pieces(x):
        return x.reshape(chunks, ROWS, blocks, size).transpose(0, 2, 1, 3)

    any_ = pl.BlockSpec(memory_space=pl.ANY)
    vmem = pl.BlockSpec(memory_space=pltpu.VMEM)
    piece = (chunks, blocks, ROWS, size)
    dma = pltpu.SemaphoreType.DMA
    peers = lax.axis_size("batch")
    ends, norms = pl.pallas_call(
        functools.partial(kernel, chain, peers),
        out_shape=(
            jax.ShapeDtypeStruct(piece, jnp.bfloat16),
            jax.ShapeDtypeStruct((ITERS,), jnp.float32),
        ),
        in_specs=[pl.BlockSpec(memory_space=pltpu.SMEM), any_, any_, any_, vmem],
        out_specs=(any_, pl.BlockSpec(memory_space=pltpu.SMEM)),
        scratch_shapes=[
            pltpu.VMEM((layers, blocks, picks * size, size), jnp.bfloat16),
            *[pltpu.VMEM(piece, jnp.bfloat16)] * 7,
            pltpu.VMEM(piece, jnp.float32),
            pltpu.VMEM((blocks, ROWS, size), jnp.bfloat16),
            *[pltpu.VMEM((blocks, QUAD * ROWS, size), jnp.bfloat16)] * 2,
            pltpu.VMEM((blocks, QUAD * ROWS, size), jnp.float32),
            *[pltpu.VMEM((blocks, rows, size), jnp.bfloat16)] * 2,
            *[pltpu.VMEM((blocks, rows, size), jnp.float32)] * 3,
            pltpu.VMEM((3, 8, BLOCK), jnp.float32),
            *[pltpu.VMEM((ITERS, 8, BLOCK), jnp.float32)] * 2,
            pltpu.VMEM((peers - 1, ITERS, 8, BLOCK), jnp.float32),
            pltpu.VMEM((ITERS, 8, BLOCK), jnp.float32),
            dma((layers,)),
            *[dma((chunks // PAIR,))] * 5,
            *[dma((chunks * CUT,))] * 4,
            dma((chunks,)),
            dma, dma, dma((peers - 1,)), dma((peers - 1,)), dma((chain - 1,)), dma,
        ],
        compiler_params=pltpu.CompilerParams(
            collective_id=0, has_side_effects=True, vmem_limit_bytes=60 << 20),
    )(
        pattern.transpose(0, 2, 1),
        pieces(inputs),
        pieces(warm_states),
        weights.reshape(layers, blocks, picks * size, size),
        bias,
    )
    ends = ends.transpose(0, 2, 1, 3).reshape(1, rows, width)
    return ends, jnp.sqrt(norms / count)


def solution(mesh):
    in_specs = (
        P("batch", None),
        P("layer", "batch", None),
        P("layer", None, None, None, None),
        P("layer", None, None),
        P("layer", None),
    )
    return jax.shard_map(
        on_device, mesh=mesh, in_specs=in_specs,
        out_specs=(P("layer", "batch", None), P()), check_vma=False)
```
